768 devices in a mesh: seq: 64 (over y, x, core), fsdp: 12 (over z).
Axes of the slice: x: 4, y: 8, z: 12, core: 2. Of those that a mesh axis runs over, the one named last changes fastest.
Arguments:
- features: bfloat16 [12, 8192, 4608], P('fsdp', 'seq'), may hold values from -6 to 6
- value_weight: bfloat16 [4608, 512], P(('seq', 'fsdp')), may hold values from -0.09375 to 0.09375
- queries: bfloat16 [12, 8192, 4096], P('fsdp', 'seq'), may hold values from -6 to 6
- key_states: bfloat16 [12, 8192, 512], P('fsdp', 'seq'), may hold values from -6 to 6
- out_grad: bfloat16 [12, 8192, 4096], P('fsdp', 'seq'), may hold values from -6 to 6
- doc_lengths: int32 [12, 64], P('fsdp'), may hold values from 1 to 256, 8192 in all within a row
Outputs:
- key_grad: bfloat16 [12, 8192, 512], P('fsdp', 'seq')
- feature_grad: bfloat16 [12, 8192, 4608], P('fsdp', 'seq')
The draws below stay inside these ranges and needn't reach their ends.
Inputs may be any that keep to these rules, and one draw needn't show every extreme that they name: `doc_lengths`: each row sums to 8192; the longest document of each row has exactly 256 tokens.
All inputs are finite; a program needn't handle non-finite values.
Results may differ from the reference program's by a relative error of at most 0.008.
Values may be sent and summed in bfloat16 or wider, within the bound.
No kernel may reach another device: no remote copies, remote signals or barrier semaphores. Data moves between devices by JAX's collectives and lax.ppermute only.
A program may use at most 64 MiB of HBM per device.

```python
import math
import jax
import jax.numpy as jnp
import numpy as np
from jax import lax

WIDTH = 4608
QHEADS = 32
KVHEADS = 4
HEAD = 128
TOK_DEV = 128
GROUP = 8
LENGTH = 8192
BATCHES = 12
NDOCS = 64
MOST = 256
N_SEQ = 64


def drawn_draw(key, width):
    return jnp.clip(jax.random.normal(key, (BATCHES, LENGTH, width), jnp.float32), -6.0, 6.0)


def draw_queries(key, part):
    drawn = drawn_draw(jax.random.fold_in(key, 1), QHEADS * HEAD)
    return drawn.astype(jnp.bfloat16)


def draw_key_states(key, part):
    drawn = drawn_draw(jax.random.fold_in(key, 2), KVHEADS * HEAD)
    return drawn.astype(jnp.bfloat16)


def block_scale(rng, dims, pieces, smallest, top_value):
    def one(axis_at, parts):
        steps = jax.random.uniform(jax.random.fold_in(jax.random.fold_in(rng, 6), axis_at), (parts,), jnp.float32, smallest / len(pieces), top_value / len(pieces))
        return jnp.repeat(jnp.exp(steps), dims[axis_at] // parts).reshape((-1,) + (1,) * (len(dims) - axis_at - 1))

    gain = one(*pieces[0])
    for cut in pieces[1:]:
        gain = gain * one(*cut)
    return gain


def length_profile(amount, total, most, lean):
    weights = [(1 << 20) // math.isqrt(rank ** lean) + 1 for rank in range(2, amount + 1)]
    surplus, given = total - most - (amount - 1), [1] * (amount - 1)
    while surplus > 0:
        free = [i for i in range(amount - 1) if given[i] < most]
        whole, remaining = sum([weights[i] for i in free]), surplus
        for i in free:
            more = min(most - given[i], max(1, remaining * weights[i] // whole), surplus)
            given[i] = given[i] + more
            surplus = surplus - more
    return np.array([most] + given)


def uneven_parts(stream_key, count, total, reach, lean):
    if count == 2:
        one = jax.random.randint(stream_key, (), max(1, total - reach), min(reach, total - 1) + 1)
        return jnp.stack([one, total - one])
    tallies = jnp.asarray(length_profile(count, total, reach, lean), jnp.int32)
    couples = (count - 1) // 2
    giver, receiver = tallies[1:1 + 2 * couples:2], tallies[2:2 + 2 * couples:2]
    margin = jnp.minimum(giver - 1, reach - receiver)
    moved = jax.random.randint(jax.random.fold_in(stream_key, 1), (couples,), 0, 1 << 20) % (margin + 1)
    tallies = tallies.at[1:1 + 2 * couples:2].set(giver - moved).at[2:2 + 2 * couples:2].set(receiver + moved)
    return tallies[jax.random.permutation(jax.random.fold_in(stream_key, 2), count)]


def scatter_about(stream_key, shape, scale, most, shards=(), held_as=jnp.bfloat16):
    values = jax.random.normal(stream_key, shape, jnp.float32) * scale
    if len(shards) > 0:
        values = block_scale(stream_key, shape, shards, -0.22, 0.18) * values
    return jnp.clip(values, min=-most, max=most).astype(held_as)


def setup_inputs(seed: int = 0) -> dict:
    key_of = jax.random.split(jax.random.key(seed), 7)
    features = scatter_about(key_of[0], (BATCHES, LENGTH, WIDTH), 1.0, 6.0, ((0, 12), (1, 64)))
    value_weight = scatter_about(key_of[1], (WIDTH, KVHEADS * HEAD), WIDTH ** -0.5, 0.09375, ((0, 768),))
    queries = draw_queries(jax.random.fold_in(key_of[6], 71), 0)
    key_states = draw_key_states(jax.random.fold_in(key_of[6], 71), 0)
    out_grad = scatter_about(key_of[4], (BATCHES, LENGTH, QHEADS * HEAD), 1.0, 6.0, ((0, 12), (1, 64)))
    doc_lengths = jax.vmap(lambda own: uneven_parts(own, NDOCS, LENGTH, MOST, 2))(jax.random.split(key_of[5], BATCHES)).reshape((BATCHES, NDOCS)).astype(jnp.int32)
    return {"features": features, "value_weight": value_weight, "queries": queries, "key_states": key_states, "out_grad": out_grad, "doc_lengths": doc_lengths}


def doc_starts(doc_lens, positions):
    doc_ends = jnp.cumsum(doc_lens).astype(jnp.int32)
    taken = jnp.where(doc_ends[None, :] <= positions[:, None], doc_lens[None, :], 0)
    return lax.optimization_barrier(jnp.sum(taken, axis=1)).astype(jnp.int32)

def block_grads(query_block, key_window, value_window, grad_block, query_pos, key_pos, starts):
    score_scale = 1.0 / math.sqrt(HEAD)
    visible = (key_pos[None, :] >= starts[:, None]) & (key_pos[None, :] <= query_pos[:, None])
    count_rows = query_block.shape[0]
    key_parts = []
    value_parts = []
    for head_index in range(KVHEADS):
        lower = head_index * GROUP * HEAD
        upper = lower + GROUP * HEAD
        query_head = query_block[:, lower:upper].reshape(count_rows, GROUP, HEAD).astype(jnp.float32)
        grad_head = grad_block[:, lower:upper].reshape(count_rows, GROUP, HEAD).astype(jnp.float32)
        key_head = key_window[:, head_index * HEAD:(head_index + 1) * HEAD].astype(jnp.float32)
        value_head = value_window[:, head_index * HEAD:(head_index + 1) * HEAD].astype(jnp.float32)
        scores = jnp.einsum('tgd,sd->gts', query_head, key_head) * score_scale
        scores = jnp.where(visible[None], scores, jnp.float32(-1e+30))
        row_max = lax.optimization_barrier(jnp.max(scores, axis=-1, keepdims=True))
        powers = jnp.exp(scores - row_max)
        probs = powers / lax.optimization_barrier(jnp.sum(powers, axis=-1, keepdims=True))
        probs_low = probs.astype(jnp.bfloat16)
        attended = jnp.einsum('gts,sd->tgd', probs_low.astype(jnp.float32), value_head)
        delta = jnp.einsum('tgd,tgd->gt', grad_head, attended)
        dprob = jnp.einsum('tgd,sd->gts', grad_head, value_head)
        dscore = (probs * (dprob - delta[:, :, None])).astype(jnp.bfloat16)
        key_part = jnp.einsum('gts,tgd->sd', dscore.astype(jnp.float32), query_head) * score_scale
        value_part = jnp.einsum('gts,tgd->sd', probs_low.astype(jnp.float32), grad_head)
        key_parts.append(key_part)
        value_parts.append(value_part)
    return (jnp.concatenate(key_parts, axis=1), jnp.concatenate(value_parts, axis=1))

def fold_windows(windows):
    span = TOK_DEV
    own_part = windows[:, 2 * span:]
    next_part = jnp.concatenate([windows[1:, span:2 * span], jnp.zeros_like(windows[:1, :span])], axis=0)
    far_part = jnp.concatenate([windows[2:, :span], jnp.zeros_like(windows[:2, :span])], axis=0)
    total = own_part + next_part + far_part
    return total.reshape(LENGTH, total.shape[-1])

def reference(features, value_weight, queries, key_states, out_grad, doc_lengths):

    def one_batch(batch_args):
        feats, query_all, key_all, grad_all, doc_lens = batch_args
        values = jnp.dot(feats, value_weight, preferred_element_type=jnp.float32).astype(jnp.bfloat16)
        key_padded = jnp.concatenate([jnp.zeros((2 * TOK_DEV, key_all.shape[1]), key_all.dtype), key_all], axis=0)
        value_padded = jnp.concatenate([jnp.zeros((2 * TOK_DEV, values.shape[1]), values.dtype), values], axis=0)
        positions = jnp.arange(LENGTH, dtype=jnp.int32)
        starts = doc_starts(doc_lens, positions)

        def one_block(block_index):
            first = (block_index * TOK_DEV).astype(jnp.int32)
            query_block = lax.dynamic_slice_in_dim(query_all, first, TOK_DEV, 0)
            grad_block = lax.dynamic_slice_in_dim(grad_all, first, TOK_DEV, 0)
            start_block = lax.dynamic_slice_in_dim(starts, first, TOK_DEV, 0)
            key_window = lax.dynamic_slice_in_dim(key_padded, first, 3 * TOK_DEV, 0)
            value_window = lax.dynamic_slice_in_dim(value_padded, first, 3 * TOK_DEV, 0)
            query_pos = first + jnp.arange(TOK_DEV, dtype=jnp.int32)
            key_pos = first - 2 * TOK_DEV + jnp.arange(3 * TOK_DEV, dtype=jnp.int32)
            return block_grads(query_block, key_window, value_window, grad_block, query_pos, key_pos, start_block)
        key_windows, value_windows = lax.map(one_block, jnp.arange(N_SEQ, dtype=jnp.int32))
        key_grad = fold_windows(key_windows).astype(jnp.bfloat16)
        value_grad = fold_windows(value_windows).astype(jnp.bfloat16)
        feature_grad = lax.dot_general(value_grad, value_weight, (((1,), (1,)), ((), ())), preferred_element_type=jnp.float32).astype(jnp.bfloat16)
        return (key_grad, feature_grad)
    key_grad, feature_grad = lax.map(one_batch, (features, queries, key_states, out_grad, doc_lengths))
    return (key_grad, feature_grad)
```

```python
import math

import jax
import jax.numpy as jnp
from jax import lax
from jax.experimental import pallas as pl
from jax.experimental.pallas import tpu as pltpu
from jax.sharding import Mesh, PartitionSpec as P

KVHEADS = 4
HEAD = 128
GROUP = 8
PAIR = 2
NEG = -1e30
VMEM_LIMIT = 12 << 20
COST = pl.CostEstimate(flops=2 * 10**9, bytes_accessed=9 * 10**6, transcendentals=2 * 10**6)


def stacked(ref, first, count):
    return jnp.concatenate(
        [ref[:, (first + i) * HEAD : (first + i + 1) * HEAD] for i in range(count)], axis=0
    )


def probs_kernel(start_ref, q_ref, g_ref, kf_ref, kn_ref, ko_ref, p_ref, vf_ref, vn_ref, vo_ref, low_ref):
    rows = q_ref.shape[0]
    keys = jnp.concatenate([kf_ref[...], kn_ref[...], ko_ref[...]], axis=0)
    shape = (3 * rows, PAIR * rows)
    key_pos = lax.broadcasted_iota(jnp.int32, shape, 0) - 2 * rows
    query_pos = lax.broadcasted_iota(jnp.int32, shape, 1) % rows
    starts = jnp.concatenate([start_ref[...]] * PAIR, axis=1)
    visible = (key_pos >= starts) & (key_pos <= query_pos)
    for pair in range(GROUP // PAIR):
        cols = slice(pair * PAIR * rows, (pair + 1) * PAIR * rows)
        query = stacked(q_ref, pair * PAIR, PAIR)
        scores = lax.dot_general(
            keys, query, (((1,), (1,)), ((), ())), preferred_element_type=jnp.float32
        ) * (1.0 / math.sqrt(HEAD))
        scores = jnp.where(visible, scores, NEG)
        powers = jnp.exp(scores - jnp.max(scores, axis=0, keepdims=True))
        probs = powers * (1.0 / jnp.sum(powers, axis=0, keepdims=True))
        p_ref[:, cols] = probs
        low_ref[:, cols] = probs.astype(jnp.bfloat16)
    part = lax.dot_general(
        low_ref[...], stacked(g_ref, 0, GROUP), (((1,), (0,)), ((), ())),
        preferred_element_type=jnp.float32,
    )
    vf_ref[...] = part[:rows].astype(vf_ref.dtype)
    vn_ref[...] = part[rows : 2 * rows].astype(vn_ref.dtype)
    vo_ref[...] = part[2 * rows :]


def grads_kernel(p_ref, q_ref, g_ref, vf_ref, vn_ref, vo_ref, kf_ref, kn_ref, ko_ref, ds_ref):
    rows = q_ref.shape[0]
    values = jnp.concatenate([vf_ref[...], vn_ref[...], vo_ref[...]], axis=0)
    for pair in range(GROUP // PAIR):
        cols = slice(pair * PAIR * rows, (pair + 1) * PAIR * rows)
        grad = stacked(g_ref, pair * PAIR, PAIR)
        dprob = lax.dot_general(
            values, grad, (((1,), (1,)), ((), ())), preferred_element_type=jnp.float32
        )
        probs = p_ref[:, cols]
        low = probs.astype(jnp.bfloat16).astype(jnp.float32)
        delta = jnp.sum(low * dprob, axis=0, keepdims=True)
        ds_ref[:, cols] = (probs * (dprob - delta)).astype(jnp.bfloat16)
    part = lax.dot_general(
        ds_ref[...], stacked(q_ref, 0, GROUP), (((1,), (0,)), ((), ())),
        preferred_element_type=jnp.float32,
    ) * (1.0 / math.sqrt(HEAD))
    kf_ref[...] = part[:rows].astype(kf_ref.dtype)
    kn_ref[...] = part[rows : 2 * rows].astype(kn_ref.dtype)
    ko_ref[...] = part[2 * rows :]


def specs(rows):
    wide = pl.BlockSpec((rows, GROUP * HEAD), lambda h: (0, h))
    head = pl.BlockSpec((rows, HEAD), lambda h: (0, h))
    probs = pl.BlockSpec((None, 3 * rows, GROUP * rows), lambda h: (h, 0, 0))
    shapes = [
        jax.ShapeDtypeStruct((rows, KVHEADS * HEAD), d) for d in (jnp.bfloat16, jnp.bfloat16, jnp.float32)
    ]
    return wide, head, probs, shapes


def probs_call(starts, query, grad, far, near, own):
    rows = query.shape[0]
    wide, head, probs, shapes = specs(rows)
    return pl.pallas_call(
        probs_kernel,
        grid=(KVHEADS,),
        in_specs=[pl.BlockSpec((1, rows), lambda h: (0, 0)), wide, wide, head, head, head],
        out_specs=[probs, head, head, head],
        out_shape=[pltpu.HBM((KVHEADS, 3 * rows, GROUP * rows), jnp.float32)] + shapes,
        scratch_shapes=[pltpu.VMEM((3 * rows, GROUP * rows), jnp.bfloat16)],
        compiler_params=pltpu.CompilerParams(vmem_limit_bytes=VMEM_LIMIT),
        cost_estimate=COST,
        name="probs",
    )(starts, query, grad, far, near, own)


def grads_call(probs_all, query, grad, far, near, own):
    rows = query.shape[0]
    wide, head, probs, shapes = specs(rows)
    return pl.pallas_call(
        grads_kernel,
        grid=(KVHEADS,),
        in_specs=[probs, wide, wide, head, head, head],
        out_specs=[head, head, head],
        out_shape=shapes,
        scratch_shapes=[pltpu.VMEM((3 * rows, GROUP * rows), jnp.bfloat16)],
        compiler_params=pltpu.CompilerParams(vmem_limit_bytes=VMEM_LIMIT),
        cost_estimate=COST,
        name="grads",
    )(probs_all, query, grad, far, near, own)


def from_behind(block, distance):
    axes = SEQ
    count = math.prod(lax.axis_size(a) for a in axes)
    route = [(i - distance, i) for i in range(count) if 0 <= i - distance < count]
    return lax.ppermute(block, axes, route)


def ring(block, axes, distance):
    count = math.prod(lax.axis_size(a) for a in axes)
    return lax.ppermute(block, axes, [(i, (i + distance) % count) for i in range(count)])


def doc_starts(doc_lens, positions):
    doc_ends = jnp.cumsum(doc_lens)
    taken = jnp.where(doc_ends[None, :] <= positions[:, None], doc_lens[None, :], 0)
    return jnp.sum(taken, axis=1)


def copies(block, axis):
    count = lax.axis_size(axis)
    return lax.all_to_all(jnp.broadcast_to(block[None], (count,) + block.shape), axis, 0, 0, tiled=True)


def gathered(weight):
    rows, width = weight.shape
    ny, nx, nc, nz = (lax.axis_size(a) for a in ("y", "x", "core", "z"))
    me, core, low = lax.axis_index("x"), lax.axis_index("core"), lax.axis_size("y") // 2
    mine = copies(weight, "z")
    mine = mine.reshape(nz * rows, width)
    mine = copies(mine, "y")
    first, second = mine[:low], mine[low:]
    left_a = ring(first, ("x",), 1)
    right_b = ring(second, ("x",), -1)
    left_b = ring(second, ("x",), 1)
    right_a = ring(first, ("x",), -1)
    far_a = ring(left_a, ("x",), 1)
    far_b = ring(right_b, ("x",), -1)
    early, late = (first, second, left_a, left_b, right_a, right_b), (far_a, far_b)
    early_swapped = ring(jnp.stack(early), ("core",), 1).reshape((3,) + mine.shape)
    late_swapped = ring(jnp.stack(late), ("core",), 1).reshape((1,) + mine.shape)
    slots = [((me + i) & (nx - 1)) * nc for i in (0, nx - 1, 1, 2)]
    whole = jnp.zeros((ny, nx * nc, nz * rows, width), weight.dtype)
    for i, piece in enumerate(early + late):
        whole = lax.dynamic_update_slice(whole, piece[:, None], (low * (i % 2), slots[i // 2] + core, 0, 0))
    for i, piece in enumerate([early_swapped[j] for j in range(3)] + [late_swapped[0]]):
        whole = lax.dynamic_update_slice(whole, piece[:, None], (0, slots[i] + 1 - core, 0, 0))
    return whole.reshape(ny * nx * nc * nz * rows, width)


def program(features, value_weight, queries, key_states, out_grad, doc_lengths):
    rows = features.shape[1]
    first = lax.axis_index(SEQ) * rows
    starts = doc_starts(doc_lengths[0], first + jnp.arange(rows, dtype=jnp.int32)) - first
    whole_weight = gathered(value_weight)
    keys = key_states[0]
    query, grad = (pltpu.with_memory_space_constraint(a[0], pltpu.HBM) for a in (queries, out_grad))
    keys_far = from_behind(keys, 2)
    keys_near = from_behind(keys, 1)
    probs, value_far, value_near, value_own = probs_call(
        starts[None], query, grad, keys_far, keys_near, keys
    )
    value_near = from_behind(value_near, -1)
    value_far = from_behind(value_far, -2)
    value_grad = (value_own + value_near + value_far).astype(jnp.bfloat16)
    values = jnp.dot(features[0], whole_weight, preferred_element_type=jnp.float32).astype(jnp.bfloat16)
    far = from_behind(values, 2)
    near = from_behind(values, 1)
    key_far, key_near, key_own = grads_call(probs, query, grad, far, near, values)
    feature_grad = lax.dot_general(
        value_grad, whole_weight, (((1,), (1,)), ((), ())), preferred_element_type=jnp.float32
    ).astype(jnp.bfloat16)
    key_far = from_behind(key_far, -2)
    key_near = from_behind(key_near, -1)
    key_grad = (key_own + key_near + key_far).astype(jnp.bfloat16)
    return (key_grad[None], feature_grad[None])


SEQ = ("y", "x", "core")


def solution(mesh):
    chips = Mesh(mesh.devices.reshape(8, 4, 2, 12), SEQ + ("z",))
    tokens = P("z", SEQ, None)
    in_specs = (tokens, P(SEQ + ("z",), None), tokens, tokens, tokens, P("z", None))
    return jax.shard_map(program, mesh=chips, in_specs=in_specs, out_specs=(tokens, tokens), check_vma=False)
```

```python
import math

import jax
import jax.numpy as jnp
from jax import lax
from jax.experimental import pallas as pl
from jax.experimental.pallas import tpu as pltpu
from jax.sharding import Mesh, PartitionSpec as P

KVHEADS = 4
HEAD = 128
GROUP = 8
PAIR = 2
NEG = -1e30
VMEM_LIMIT = 12 << 20
COST = pl.CostEstimate(flops=2 * 10**9, bytes_accessed=9 * 10**6, transcendentals=2 * 10**6)


def stacked(ref, first, count):
    return jnp.concatenate(
        [ref[:, (first + i) * HEAD : (first + i + 1) * HEAD] for i in range(count)], axis=0
    )


def probs_kernel(start_ref, q_ref, g_ref, kf_ref, kn_ref, ko_ref, p_ref, vf_ref, vn_ref, vo_ref, low_ref):
    rows = q_ref.shape[0]
    keys = jnp.concatenate([kf_ref[...], kn_ref[...], ko_ref[...]], axis=0)
    shape = (3 * rows, PAIR * rows)
    key_pos = lax.broadcasted_iota(jnp.int32, shape, 0) - 2 * rows
    query_pos = lax.broadcasted_iota(jnp.int32, shape, 1) % rows
    starts = jnp.concatenate([start_ref[...]] * PAIR, axis=1)
    visible = (key_pos >= starts) & (key_pos <= query_pos)
    for pair in range(GROUP // PAIR):
        cols = slice(pair * PAIR * rows, (pair + 1) * PAIR * rows)
        query = stacked(q_ref, pair * PAIR, PAIR)
        scores = lax.dot_general(
            keys, query, (((1,), (1,)), ((), ())), preferred_element_type=jnp.float32
        ) * (1.0 / math.sqrt(HEAD))
        scores = jnp.where(visible, scores, NEG)
        powers = jnp.exp(scores - jnp.max(scores, axis=0, keepdims=True))
        probs = powers * (1.0 / jnp.sum(powers, axis=0, keepdims=True))
        p_ref[:, cols] = probs
        low_ref[:, cols] = probs.astype(jnp.bfloat16)
    part = lax.dot_general(
        low_ref[...], stacked(g_ref, 0, GROUP), (((1,), (0,)), ((), ())),
        preferred_element_type=jnp.float32,
    )
    vf_ref[...] = part[:rows].astype(vf_ref.dtype)
    vn_ref[...] = part[rows : 2 * rows].astype(vn_ref.dtype)
    vo_ref[...] = part[2 * rows :]


def grads_kernel(p_ref, q_ref, g_ref, vf_ref, vn_ref, vo_ref, kf_ref, kn_ref, ko_ref, ds_ref):
    rows = q_ref.shape[0]
    values = jnp.concatenate([vf_ref[...], vn_ref[...], vo_ref[...]], axis=0)
    for pair in range(GROUP // PAIR):
        cols = slice(pair * PAIR * rows, (pair + 1) * PAIR * rows)
        grad = stacked(g_ref, pair * PAIR, PAIR)
        dprob = lax.dot_general(
            values, grad, (((1,), (1,)), ((), ())), preferred_element_type=jnp.float32
        )
        probs = p_ref[:, cols]
        low = probs.astype(jnp.bfloat16).astype(jnp.float32)
        delta = jnp.sum(low * dprob, axis=0, keepdims=True)
        ds_ref[:, cols] = (probs * (dprob - delta)).astype(jnp.bfloat16)
    part = lax.dot_general(
        ds_ref[...], stacked(q_ref, 0, GROUP), (((1,), (0,)), ((), ())),
        preferred_element_type=jnp.float32,
    ) * (1.0 / math.sqrt(HEAD))
    kf_ref[...] = part[:rows].astype(kf_ref.dtype)
    kn_ref[...] = part[rows : 2 * rows].astype(kn_ref.dtype)
    ko_ref[...] = part[2 * rows :]


def specs(rows):
    wide = pl.BlockSpec((rows, GROUP * HEAD), lambda h: (0, h))
    head = pl.BlockSpec((rows, HEAD), lambda h: (0, h))
    probs = pl.BlockSpec((None, 3 * rows, GROUP * rows), lambda h: (h, 0, 0))
    shapes = [
        jax.ShapeDtypeStruct((rows, KVHEADS * HEAD), d) for d in (jnp.bfloat16, jnp.bfloat16, jnp.float32)
    ]
    return wide, head, probs, shapes


def probs_call(starts, query, grad, far, near, own):
    rows = query.shape[0]
    wide, head, probs, shapes = specs(rows)
    return pl.pallas_call(
        probs_kernel,
        grid=(KVHEADS,),
        in_specs=[pl.BlockSpec((1, rows), lambda h: (0, 0)), wide, wide, head, head, head],
        out_specs=[probs, head, head, head],
        out_shape=[pltpu.HBM((KVHEADS, 3 * rows, GROUP * rows), jnp.float32)] + shapes,
        scratch_shapes=[pltpu.VMEM((3 * rows, GROUP * rows), jnp.bfloat16)],
        compiler_params=pltpu.CompilerParams(vmem_limit_bytes=VMEM_LIMIT),
        cost_estimate=COST,
        name="probs",
    )(starts, query, grad, far, near, own)


def grads_call(probs_all, query, grad, far, near, own):
    rows = query.shape[0]
    wide, head, probs, shapes = specs(rows)
    return pl.pallas_call(
        grads_kernel,
        grid=(KVHEADS,),
        in_specs=[probs, wide, wide, head, head, head],
        out_specs=[head, head, head],
        out_shape=shapes,
        scratch_shapes=[pltpu.VMEM((3 * rows, GROUP * rows), jnp.bfloat16)],
        compiler_params=pltpu.CompilerParams(vmem_limit_bytes=VMEM_LIMIT),
        cost_estimate=COST,
        name="grads",
    )(probs_all, query, grad, far, near, own)


def from_behind(block, distance):
    axes = SEQ
    count = math.prod(lax.axis_size(a) for a in axes)
    route = [(i - distance, i) for i in range(count) if 0 <= i - distance < count]
    return lax.ppermute(block, axes, route)


def ring(block, axes, distance):
    count = math.prod(lax.axis_size(a) for a in axes)
    return lax.ppermute(block, axes, [(i, (i + distance) % count) for i in range(count)])


def doc_starts(doc_lens, positions):
    doc_ends = jnp.cumsum(doc_lens)
    taken = jnp.where(doc_ends[None, :] <= positions[:, None], doc_lens[None, :], 0)
    return jnp.sum(taken, axis=1)


def copies(block, axes, count, groups=None):
    stacked_copies = jnp.broadcast_to(block[None], (count,) + block.shape)
    return lax.all_to_all(stacked_copies, axes, 0, 0, axis_index_groups=groups, tiled=True)


def gathered(weight):
    rows, width = weight.shape
    ny, nx, nc, nz = (lax.axis_size(a) for a in ("y", "x", "core", "z"))
    y, x, core = (lax.axis_index(a) for a in ("y", "x", "core"))
    order = [*range(0, ny, 2), *range(1, ny, 2)]
    groups = [[row * nx + (c + 2 * (row % 2)) % nx for row in order] for c in range(nx)]
    mine = copies(weight, "z", nz)
    mine = mine.reshape(nz * rows, width)
    mine = copies(mine, ("y", "x"), ny, groups)
    above = ring(mine, ("y",), 1)
    left = ring(mine, ("x",), 1)
    right = ring(mine, ("x",), -1)
    blocks, offsets = (mine, above, left, right), (0, 2, nx - 1, 1)
    swapped = ring(jnp.stack(blocks[:2]), ("core",), 1)
    late = ring(jnp.stack(blocks[2:]), ("core",), 1)
    whole = jnp.zeros((ny // 2, 2, nx * nc, nz * rows, width), weight.dtype)
    pieces = [(b, o, core) for b, o in zip(blocks, offsets)]
    pieces += [(b, o, 1 - core) for b, o in zip((swapped[0], swapped[1], late[0], late[1]), offsets)]
    for block, offset, side in pieces:
        color = x + 2 * (y % 2) + offset
        for odd in range(2):
            half = block[odd * ny // 2 : (odd + 1) * ny // 2, None, None]
            slot = ((color + 2 * odd) & (nx - 1)) * nc + side
            whole = lax.dynamic_update_slice(whole, half, (0, odd, slot, 0, 0))
    return whole.reshape(ny * nx * nc * nz * rows, width)


def program(features, value_weight, queries, key_states, out_grad, doc_lengths):
    rows = features.shape[1]
    first = lax.axis_index(SEQ) * rows
    starts = doc_starts(doc_lengths[0], first + jnp.arange(rows, dtype=jnp.int32)) - first
    whole_weight = gathered(value_weight)
    keys = key_states[0]
    query, grad, own_keys = (
        pltpu.with_memory_space_constraint(a[0], pltpu.HBM) for a in (queries, out_grad, key_states)
    )
    keys_far = from_behind(keys, 2)
    keys_near = from_behind(keys, 1)
    probs, value_far, value_near, value_own = probs_call(
        starts[None], query, grad, keys_far, keys_near, own_keys
    )
    value_near = from_behind(value_near, -1)
    value_far = from_behind(value_far, -2)
    value_grad = (value_own + value_near + value_far).astype(jnp.bfloat16)
    values = jnp.dot(features[0], whole_weight, preferred_element_type=jnp.float32).astype(jnp.bfloat16)
    far = from_behind(values, 2)
    near = from_behind(values, 1)
    key_far, key_near, key_own = grads_call(probs, queries[0], out_grad[0], far, near, values)
    feature_grad = lax.dot_general(
        value_grad, whole_weight, (((1,), (1,)), ((), ())), preferred_element_type=jnp.float32
    ).astype(jnp.bfloat16)
    key_far = from_behind(key_far, -2)
    key_near = from_behind(key_near, -1)
    key_grad = (key_own + key_near + key_far).astype(jnp.bfloat16)
    return (key_grad[None], feature_grad[None])


SEQ = ("y", "x", "core")


def solution(mesh):
    chips = Mesh(mesh.devices.reshape(8, 4, 2, 12), SEQ + ("z",))
    tokens = P("z", SEQ, None)
    in_specs = (tokens, P(SEQ + ("z",), None), tokens, tokens, tokens, P("z", None))
    return jax.shard_map(program, mesh=chips, in_specs=in_specs, out_specs=(tokens, tokens), check_vma=False)
```
